32 devices in a mesh: fsdp: 32 (over z, y, x, core).
Axes of the slice: x: 2, y: 2, z: 4, core: 2. Of those that a mesh axis runs over, the one named last changes fastest.
Arguments:
- decoder_in: bfloat16 [65536, 512], P('fsdp'), may hold values from -12 to 12
- memory: bfloat16 [16384, 512], P('fsdp'), may hold values from -12 to 12
- cotangent: bfloat16 [65536, 512], P('fsdp'), may hold values from -12 to 12
- self_query: bfloat16 [512, 512], P('fsdp'), may hold values from -0.25 to 0.25
- self_query_bias: bfloat16 [512], P('fsdp'), may hold values from -1.25 to 1.25
- self_key: bfloat16 [512, 512], P('fsdp'), may hold values from -0.25 to 0.25
- self_value: bfloat16 [512, 512], P('fsdp'), may hold values from -0.25 to 0.25
- self_value_bias: bfloat16 [512], P('fsdp'), may hold values from -1.25 to 1.25
- self_output: bfloat16 [512, 512], P('fsdp'), may hold values from -2 to 2
- self_output_bias: bfloat16 [512], P('fsdp'), may hold values from -1.25 to 1.25
- first_gain: bfloat16 [512], P('fsdp'), may hold values from 0.5 to 1.5
- first_shift: bfloat16 [512], P('fsdp'), may hold values from -1.25 to 1.25
- cross_query: bfloat16 [512, 512], P('fsdp'), may hold values from -0.25 to 0.25
- cross_query_bias: bfloat16 [512], P('fsdp'), may hold values from -1.25 to 1.25
- cross_key: bfloat16 [512, 512], P('fsdp'), may hold values from -0.25 to 0.25
- cross_value: bfloat16 [512, 512], P('fsdp'), may hold values from -0.25 to 0.25
- cross_value_bias: bfloat16 [512], P('fsdp'), may hold values from -1.25 to 1.25
- cross_output: bfloat16 [512, 512], P('fsdp'), may hold values from -2 to 2
- cross_output_bias: bfloat16 [512], P('fsdp'), may hold values from -1.25 to 1.25
- second_gain: bfloat16 [512], P('fsdp'), may hold values from 0.5 to 1.5
- second_shift: bfloat16 [512], P('fsdp'), may hold values from -1.25 to 1.25
- expand_weight: bfloat16 [512, 2048], P('fsdp'), may hold values from -0.25 to 0.25
- expand_bias: bfloat16 [2048], P('fsdp'), may hold values from -1.25 to 1.25
- contract_weight: bfloat16 [2048, 512], P('fsdp'), may hold values from -0.25 to 0.25
- contract_bias: bfloat16 [512], P('fsdp'), may hold values from -1.25 to 1.25
- third_gain: bfloat16 [512], P('fsdp'), may hold values from 0.5 to 1.5
- third_shift: bfloat16 [512], P('fsdp'), may hold values from -1.25 to 1.25
Outputs:
- decoder_out: bfloat16 [65536, 512], P('fsdp')
- input_grad: float32 [65536, 512], P('fsdp')
- memory_grad: float32 [16384, 512], P('fsdp')
- self_query_grad: float32 [512, 512], P('fsdp')
- self_query_bias_grad: float32 [512], P('fsdp')
- self_key_grad: float32 [512, 512], P('fsdp')
- self_value_grad: float32 [512, 512], P('fsdp')
- self_value_bias_grad: float32 [512], P('fsdp')
- self_output_grad: float32 [512, 512], P('fsdp')
- self_output_bias_grad: float32 [512], P('fsdp')
- first_gain_grad: float32 [512], P('fsdp')
- first_shift_grad: float32 [512], P('fsdp')
- cross_query_grad: float32 [512, 512], P('fsdp')
- cross_query_bias_grad: float32 [512], P('fsdp')
- cross_key_grad: float32 [512, 512], P('fsdp')
- cross_value_grad: float32 [512, 512], P('fsdp')
- cross_value_bias_grad: float32 [512], P('fsdp')
- cross_output_grad: float32 [512, 512], P('fsdp')
- cross_output_bias_grad: float32 [512], P('fsdp')
- second_gain_grad: float32 [512], P('fsdp')
- second_shift_grad: float32 [512], P('fsdp')
- expand_weight_grad: float32 [512, 2048], P('fsdp')
- expand_bias_grad: float32 [2048], P('fsdp')
- contract_weight_grad: float32 [2048, 512], P('fsdp')
- contract_bias_grad: float32 [512], P('fsdp')
- third_gain_grad: float32 [512], P('fsdp')
- third_shift_grad: float32 [512], P('fsdp')
The draws below stay inside these ranges and needn't reach their ends.
All inputs are finite; a program needn't handle non-finite values.
Results may differ from the reference program's by a relative error of at most 0.03.
Values may be sent and summed in bfloat16 or wider, within the bound.
No kernel may reach another device: no remote copies, remote signals or barrier semaphores. Data moves between devices by JAX's collectives and lax.ppermute only.
A program may use at most 384 MiB of HBM per device.

```python
import jax
import jax.numpy as jnp
from jax import lax

D = 512
HEADS = 8
FF = 2048
LEN = 2048
SRC = 512
TOKENS = 65536
MEM_ROWS = 16384


def with_spikes(result, own_key, source, target, parts, factor):
    owner, partner = [(jnp.arange(result.shape[position]) // (result.shape[position] // parts)).reshape([-1 if axis == position else 1 for axis in range(result.ndim)]) for position in (source, target)]
    chosen = jax.random.permutation(own_key, parts)[partner]
    strong = (owner == chosen) | (owner == (partner + parts // 2) % parts)
    return jnp.where(strong, factor * result, result)


def shard_levels(stream_key, dims, shards, least, high):
    level, own = 1.0, jax.random.fold_in(stream_key, 6)
    for position, shards_of in shards:
        draws = jnp.exp(jax.random.uniform(jax.random.fold_in(own, position), (shards_of,), jnp.float32, least / len(shards), high / len(shards)))
        level = level * jnp.repeat(draws, dims[position] // shards_of).reshape([-1 if axis == position else 1 for axis in range(len(dims))])
    return level


def noise(key, dims, scale, bound, cuts=(), kind=jnp.bfloat16):
    values = jax.random.normal(key, dims, jnp.float32) * scale
    if len(cuts) > 0:
        values = shard_levels(key, dims, cuts, -0.22, 0.18) * values
    return jnp.clip(values, min=-bound, max=bound).astype(kind)


def noise_with(rng, extent, spread, reach, shards, heavy, held_as=jnp.bfloat16):
    result = spread * jax.random.normal(rng, extent, jnp.float32)
    if shards:
        result = result * shard_levels(rng, extent, shards, -0.22, 0.18)
    return jnp.clip(with_spikes(result, jax.random.fold_in(rng, 3), *heavy), -reach, reach).astype(held_as)


def setup_inputs(seed: int = 0) -> dict:
    key_of = jax.random.split(jax.random.key(seed), 28)
    return {
        "decoder_in": noise_with(key_of[0], (TOKENS, D), 1.0, 12.0, ((0, 32),), (0, 1, 32, 2.75)),
        "memory": noise_with(key_of[1], (MEM_ROWS, D), 1.0, 12.0, ((0, 32),), (0, 1, 32, 2.75)),
        "cotangent": noise_with(key_of[2], (TOKENS, D), 1.0, 12.0, ((0, 32),), (0, 1, 32, 2.75)),
        "self_query": noise(key_of[3], (D, D), D ** -0.5, 0.25, ((0, 32),)),
        "self_query_bias": noise(key_of[4], (D,), 0.2, 1.25, ((0, 32),)),
        "self_key": noise(key_of[5], (D, D), D ** -0.5, 0.25, ((0, 32),)),
        "self_value": noise(key_of[6], (D, D), D ** -0.5, 0.25, ((0, 32),)),
        "self_value_bias": noise(key_of[7], (D,), 0.2, 1.25, ((0, 32),)),
        "self_output": noise(key_of[8], (D, D), (D // 64) ** -0.5, 2.0, ((0, 32),)),
        "self_output_bias": noise(key_of[9], (D,), 0.2, 1.25, ((0, 32),)),
        "first_gain": jnp.clip(1.0 + 0.1 * jax.random.normal(key_of[10], (D,), jnp.float32), 0.5, 1.5).astype(jnp.bfloat16),
        "first_shift": noise(key_of[11], (D,), 0.2, 1.25, ((0, 32),)),
        "cross_query": noise(key_of[12], (D, D), D ** -0.5, 0.25, ((0, 32),)),
        "cross_query_bias": noise(key_of[13], (D,), 0.2, 1.25, ((0, 32),)),
        "cross_key": noise(key_of[14], (D, D), D ** -0.5, 0.25, ((0, 32),)),
        "cross_value": noise(key_of[15], (D, D), D ** -0.5, 0.25, ((0, 32),)),
        "cross_value_bias": noise(key_of[16], (D,), 0.2, 1.25, ((0, 32),)),
        "cross_output": noise(key_of[17], (D, D), (D // 64) ** -0.5, 2.0, ((0, 32),)),
        "cross_output_bias": noise(key_of[18], (D,), 0.2, 1.25, ((0, 32),)),
        "second_gain": jnp.clip(1.0 + 0.1 * jax.random.normal(key_of[19], (D,), jnp.float32), 0.5, 1.5).astype(jnp.bfloat16),
        "second_shift": noise(key_of[20], (D,), 0.2, 1.25, ((0, 32),)),
        "expand_weight": noise(key_of[21], (D, FF), D ** -0.5, 0.25, ((0, 32),)),
        "expand_bias": noise(key_of[22], (FF,), 0.2, 1.25, ((0, 32),)),
        "contract_weight": noise(key_of[23], (FF, D), (FF // 4) ** -0.5, 0.25, ((0, 32),)),
        "contract_bias": noise(key_of[24], (D,), 0.2, 1.25, ((0, 32),)),
        "third_gain": jnp.clip(1.0 + 0.1 * jax.random.normal(key_of[25], (D,), jnp.float32), 0.5, 1.5).astype(jnp.bfloat16),
        "third_shift": noise(key_of[26], (D,), 0.2, 1.25, ((0, 32),)),
    }


epsilon = 1e-05

@jax.custom_vjp
def low(v):
    return lax.optimization_barrier(v.astype(jnp.bfloat16)).astype(jnp.float32)

@jax.custom_vjp
def low_back(v):
    return v

def low_keep(v):
    return (low(v), None)

def low_pass(kept, grad):
    return (grad,)

def back_keep(v):
    return (v, None)

def back_low(kept, grad):
    return (low(grad),)
low.defvjp(low_keep, low_pass)
low_back.defvjp(back_keep, back_low)

def matmul_high(left, right):
    return jnp.dot(left, right, precision=lax.Precision.HIGHEST)

def layer_norm(summed, gain, shift):
    row_mean = lax.optimization_barrier(jnp.mean(summed, axis=-1, keepdims=True))
    centred = summed - row_mean
    variance = lax.optimization_barrier(jnp.mean(centred * centred, axis=-1, keepdims=True))
    return centred * lax.rsqrt(variance + epsilon) * gain + shift

def attend(query_low, key_low, value_low, causal):
    length = query_low.shape[0]
    keys_count = key_low.shape[0]
    head_dim = query_low.shape[1] // HEADS
    query_heads = query_low.reshape(length, HEADS, head_dim)
    key_heads = key_low.reshape(keys_count, HEADS, head_dim)
    value_heads = value_low.reshape(keys_count, HEADS, head_dim)
    scores = jnp.einsum('qhd,khd->hqk', query_heads, key_heads, precision=lax.Precision.HIGHEST) * head_dim ** (-0.5)
    scores = low_back(scores)
    if causal:
        allowed = jnp.arange(keys_count)[None, :] <= jnp.arange(length)[:, None]
        scores = jnp.where(allowed[None], scores, -1e+30)
    weights_low = low(jax.nn.softmax(scores, axis=-1))
    context = jnp.einsum('hqk,khd->qhd', weights_low, value_heads, precision=lax.Precision.HIGHEST)
    return low(low_back(context.reshape(length, -1)))

def forward(seq_in, seq_mem, params):
    self_query, self_query_bias, self_key, self_value, self_value_bias, self_output, self_output_bias, first_gain, first_shift, cross_query, cross_query_bias, cross_key, cross_value, cross_value_bias, cross_output, cross_output_bias, second_gain, second_shift, expand_weight, expand_bias, contract_weight, contract_bias, third_gain, third_shift = params
    query_low = low(low_back(matmul_high(seq_in, self_query) + self_query_bias))
    key_low = low(low_back(matmul_high(seq_in, self_key)))
    value_low = low(low_back(matmul_high(seq_in, self_value) + self_value_bias))
    context = attend(query_low, key_low, value_low, True)
    self_branch = low_back(matmul_high(context, self_output) + self_output_bias)
    first_out = layer_norm(seq_in + self_branch, first_gain, first_shift)
    first_low = low(first_out)
    cross_q = low(low_back(matmul_high(first_low, cross_query) + cross_query_bias))
    cross_k = low(low_back(matmul_high(seq_mem, cross_key)))
    cross_v = low(low_back(matmul_high(seq_mem, cross_value) + cross_value_bias))
    cross_context = attend(cross_q, cross_k, cross_v, False)
    cross_branch = low_back(matmul_high(cross_context, cross_output) + cross_output_bias)
    second_out = layer_norm(first_out + cross_branch, second_gain, second_shift)
    second_low = low(second_out)
    gate_pre = low_back(matmul_high(second_low, expand_weight) + expand_bias)
    hidden = low(jax.nn.silu(gate_pre))
    ffn_branch = low_back(matmul_high(hidden, contract_weight) + contract_bias)
    return layer_norm(second_out + ffn_branch, third_gain, third_shift)

def reference(decoder_in, memory, cotangent, self_query, self_query_bias, self_key, self_value, self_value_bias, self_output, self_output_bias, first_gain, first_shift, cross_query, cross_query_bias, cross_key, cross_value, cross_value_bias, cross_output, cross_output_bias, second_gain, second_shift, expand_weight, expand_bias, contract_weight, contract_bias, third_gain, third_shift):
    params = tuple((p.astype(jnp.float32) for p in (self_query, self_query_bias, self_key, self_value, self_value_bias, self_output, self_output_bias, first_gain, first_shift, cross_query, cross_query_bias, cross_key, cross_value, cross_value_bias, cross_output, cross_output_bias, second_gain, second_shift, expand_weight, expand_bias, contract_weight, contract_bias, third_gain, third_shift)))
    count = decoder_in.shape[0] // LEN
    inputs = decoder_in.astype(jnp.float32).reshape(count, LEN, D)
    memories = memory.astype(jnp.float32).reshape(count, SRC, D)
    cotangents = cotangent.astype(jnp.float32).reshape(count, LEN, D)

    def step(totals, seq_items):
        seq_in, seq_mem, seq_cot = seq_items
        seq_out, pull_back = jax.vjp(forward, seq_in, seq_mem, params)
        grad_in, grad_mem, grad_params = pull_back(seq_cot)
        totals = jax.tree.map(lambda t, g: t + g, totals, grad_params)
        return (totals, (seq_out.astype(jnp.bfloat16), grad_in, grad_mem))
    totals, (outputs, input_grads, memory_grads) = lax.scan(step, jax.tree.map(jnp.zeros_like, params), (inputs, memories, cotangents))
    return (outputs.reshape(count * LEN, D), input_grads.reshape(count * LEN, D), memory_grads.reshape(count * SRC, D), totals[0], totals[1], totals[2], totals[3], totals[4], totals[5], totals[6], totals[7], totals[8], totals[9], totals[10], totals[11], totals[12], totals[13], totals[14], totals[15], totals[16], totals[17], totals[18], totals[19], totals[20], totals[21], totals[22], totals[23])
```

```python
import functools

import jax
import jax.numpy as jnp
from jax import lax
from jax.experimental import pallas as pl
from jax.experimental.pallas import tpu as pltpu
from jax.sharding import PartitionSpec as P

HEADS = 8
EPS = 1e-05
BF = jnp.bfloat16
F32 = jnp.float32
QB = 256
ROWS = 256

VECS = (
    "sqb", "svb", "sob", "g1", "b1", "cqb", "cvb", "cob", "g2", "b2", "cb", "g3", "b3",
)
EB_ROW = len(VECS)
ROW_OF = {name: row for row, name in enumerate(VECS)}


def dot_nn(a, b):
    return lax.dot_general(a, b, (((1,), (0,)), ((), ())), preferred_element_type=F32)


def dot_nt(a, b):
    return lax.dot_general(a, b, (((1,), (1,)), ((), ())), preferred_element_type=F32)


def dot_tn(a, b):
    return lax.dot_general(a, b, (((0,), (0,)), ((), ())), preferred_element_type=F32)


def stage_sizes(n):
    sizes = []
    while n > 4:
        sizes.append(2)
        n //= 2
    return (n, *sizes)


def strides_of(sizes):
    strides, stride = [], 1
    for size in reversed(sizes):
        strides.append(stride)
        stride *= size
    return tuple(reversed(strides))


def shift_perm(n, stride, size, by):
    pairs = []
    for source in range(n):
        digit = (source // stride) % size
        pairs.append((source, source + ((digit + by) % size - digit) * stride))
    return pairs


def gather_rows(block, n):
    sizes = stage_sizes(n)
    strides = strides_of(sizes)
    index = lax.axis_index("fsdp")
    size, stride = sizes[0], strides[0]
    digit = (index // stride) % size
    pieces = [block]
    for by in range(1, size):
        pieces.append(lax.ppermute(block, "fsdp", shift_perm(n, stride, size, by)))
    table = jnp.stack([pieces[(size - 1 - t) % size] for t in range(2 * size - 1)])
    whole = lax.dynamic_slice_in_dim(table, size - 1 - digit, size, 0)
    for size, stride in zip(sizes[1:], strides[1:]):
        digit = (index // stride) % size
        other = lax.ppermute(whole, "fsdp", shift_perm(n, stride, size, 1))
        first = jnp.where(digit == 0, whole, other)
        second = jnp.where(digit == 0, other, whole)
        whole = jnp.stack([first, second], axis=1)
        whole = whole.reshape((-1,) + block.shape)
    return whole


def scatter_rows(partial, n):
    sizes = stage_sizes(n)
    strides = strides_of(sizes)
    index = lax.axis_index("fsdp")
    rest = partial
    for size, stride in reversed(list(zip(sizes[1:], strides[1:]))):
        digit = (index // stride) % size
        pairs = rest.reshape((-1, 2) + rest.shape[1:])
        send = lax.dynamic_index_in_dim(pairs, 1 - digit, 1, False)
        keep = lax.dynamic_index_in_dim(pairs, digit, 1, False)
        got = lax.ppermute(send, "fsdp", shift_perm(n, stride, size, 1))
        rest = (keep.astype(F32) + got.astype(F32)).astype(BF)
    size, stride = sizes[0], strides[0]
    digit = (index // stride) % size
    total = lax.dynamic_index_in_dim(rest, digit, 0, False).astype(F32)
    for by in range(1, size):
        send = lax.dynamic_index_in_dim(rest, (digit + by) % size, 0, False)
        got = lax.ppermute(send, "fsdp", shift_perm(n, stride, size, by))
        total = total + got.astype(F32)
    return total


def pair_masks(rows):
    lane = lax.broadcasted_iota(jnp.int32, (rows, 128), 1)
    return lane < 64


def self_forward_kernel(q_ref, k_ref, v_ref, o_ref, lse_ref):
    length = q_ref.shape[0]
    keys = k_ref[...]
    vt = v_ref[...].T
    top = lax.broadcasted_iota(jnp.int32, vt.shape, 0) < 64
    ones = jnp.ones_like(vt)
    vt_heads = (jnp.where(top, vt, ones), jnp.where(top, ones, vt))
    first_half = pair_masks(QB)
    keep = lax.broadcasted_iota(jnp.int32, (QB, QB), 0) <= lax.broadcasted_iota(
        jnp.int32, (QB, QB), 1
    )
    for start in range(0, length, QB):
        end = start + QB
        query = q_ref[start:end, :] * jnp.asarray(0.125, BF)
        zeros = jnp.zeros_like(query)
        parts, logs = [], []
        for head in range(2):
            own = jnp.where(first_half if head == 0 else ~first_half, query, zeros)
            last = jnp.where(keep, dot_nt(keys[start:end], own), -1e30)
            peak = jnp.max(last, axis=0, keepdims=True)
            if start:
                scores = dot_nt(keys[:start], own)
                peak = jnp.maximum(peak, jnp.max(scores, axis=0, keepdims=True))
            expd = jnp.exp(last - peak).astype(BF)
            acc = dot_nn(vt_heads[head][:, start:end], expd)
            if start:
                expd = jnp.exp(scores - peak).astype(BF)
                acc = acc + dot_nn(vt_heads[head][:, :start], expd)
            if head == 0:
                total = acc[64:65]
                parts.append(acc[:64] / total)
            else:
                total = acc[:1]
                parts.append(acc[64:] / total)
            logs.append(peak + jnp.log(total))
        context = jnp.concatenate(parts, axis=0)
        o_ref[start:end, :] = context.T.astype(BF)
        lse_ref[0, :, start:end] = jnp.concatenate(logs, axis=0)


def self_forward(query, key, value):
    length, width = query.shape
    pairs = width // 128
    spec = pl.BlockSpec((length, 128), lambda p: (0, p))
    area = length * length // 2
    return pl.pallas_call(
        self_forward_kernel,
        grid=(pairs,),
        in_specs=[spec, spec, spec],
        out_specs=[spec, pl.BlockSpec((1, 2, length), lambda p: (p, 0, 0))],
        out_shape=[
            jax.ShapeDtypeStruct((length, width), BF),
            jax.ShapeDtypeStruct((pairs, 2, length), F32),
        ],
        cost_estimate=pl.CostEstimate(
            flops=4 * area * width * 4, bytes_accessed=8 * length * width,
            transcendentals=area * HEADS,
        ),
        name="self_forward",
    )(query, key, value)


def self_backward_kernel(
    q_ref, k_ref, v_ref, o_ref, g_ref, lse_ref, dq_ref, dk_ref, dv_ref, dk_acc, dv_acc
):
    length = q_ref.shape[0]
    keys = k_ref[...]
    values = v_ref[...]
    kt = keys.T
    first_half = pair_masks(QB)
    top = lax.broadcasted_iota(jnp.int32, (128, QB), 0) < 64
    keep = lax.broadcasted_iota(jnp.int32, (QB, QB), 0) <= lax.broadcasted_iota(
        jnp.int32, (QB, QB), 1
    )
    for start in range(0, length, QB):
        end = start + QB
        query = q_ref[start:end, :] * jnp.asarray(0.125, BF)
        grad = g_ref[start:end, :]
        inner = (grad.astype(F32) * o_ref[start:end, :].astype(F32)).T
        zeros = jnp.zeros_like(query)
        weights_of, scores_of, own_q, own_g, dq_parts = [], [], [], [], []
        for head in range(2):
            mine = first_half if head == 0 else ~first_half
            own = jnp.where(mine, query, zeros)
            own_grad = jnp.where(mine, grad, zeros)
            delta = jnp.sum(inner[head * 64 : head * 64 + 64], axis=0, keepdims=True)
            log_sum = lse_ref[0, head : head + 1, start:end]
            scores = dot_nt(keys[:end], own)
            if start:
                scores = jnp.concatenate(
                    [scores[:start], jnp.where(keep, scores[start:], -1e30)], axis=0
                )
            else:
                scores = jnp.where(keep, scores, -1e30)
            probs = jnp.exp(scores - log_sum)
            prob_grad = dot_nt(values[:end], own_grad)
            score_low = (probs * (prob_grad - delta)).astype(BF)
            dq_parts.append(dot_nn(kt[:, :end], score_low))
            weights_of.append(probs.astype(BF))
            scores_of.append(score_low)
            own_q.append(own)
            own_g.append(own_grad)
        dq = jnp.where(top, dq_parts[0], dq_parts[1]) * 0.125
        dq_ref[start:end, :] = dq.T.astype(BF)
        dk = dot_nn(scores_of[0], own_q[0]) + dot_nn(scores_of[1], own_q[1])
        dv = dot_nn(weights_of[0], own_g[0]) + dot_nn(weights_of[1], own_g[1])
        if start:
            dk_acc[:start, :] += dk[:start]
            dv_acc[:start, :] += dv[:start]
        dk_acc[start:end, :] = dk[start:]
        dv_acc[start:end, :] = dv[start:]
    dk_ref[...] = dk_acc[...].astype(BF)
    dv_ref[...] = dv_acc[...].astype(BF)


def self_backward(query, key, value, context, grad, log_sum):
    length, width = query.shape
    pairs = width // 128
    spec = pl.BlockSpec((length, 128), lambda p: (0, p))
    area = length * length // 2
    shape = jax.ShapeDtypeStruct((length, width), BF)
    return pl.pallas_call(
        self_backward_kernel,
        grid=(pairs,),
        in_specs=[spec] * 5 + [pl.BlockSpec((1, 2, length), lambda p: (p, 0, 0))],
        out_specs=[spec, spec, spec],
        out_shape=[shape, shape, shape],
        scratch_shapes=[pltpu.VMEM((length, 128), F32), pltpu.VMEM((length, 128), F32)],
        cost_estimate=pl.CostEstimate(
            flops=10 * area * width * 4, bytes_accessed=16 * length * width,
            transcendentals=area * HEADS,
        ),
        name="self_backward",
    )(query, key, value, context, grad, log_sum)


def norm(summed, gain, shift):
    mean = jnp.mean(summed, axis=-1, keepdims=True)
    centred = summed - mean
    inverse = lax.rsqrt(jnp.mean(centred * centred, axis=-1, keepdims=True) + EPS)
    normed = centred * inverse
    return normed * gain + shift, normed, inverse


def norm_back(incoming, normed, inverse, gain):
    scaled = incoming * gain
    return inverse * (
        scaled
        - jnp.mean(scaled, axis=-1, keepdims=True)
        - normed * jnp.mean(scaled * normed, axis=-1, keepdims=True)
    )


def col_sum(value):
    return jnp.sum(value.astype(F32), axis=0, keepdims=True)


def middle_kernel(
    x_ref, ctx_ref, cot_ref, k_ref, v_ref, so_ref, cq_ref, co_ref, ew_ref, cw_ref, vec_ref,
    out_ref, fsg_ref, scl_ref,
    dso_ref, dcq_ref, dco_ref, dew_ref, dcw_ref, dk_ref, dv_ref, dvec_ref,
    expd_ref,
):
    step = pl.program_id(0)
    width = x_ref.shape[1]
    inner = ew_ref.shape[1]
    pairs = width // 128
    rows = x_ref.shape[0]

    @pl.when(step == 0)
    def _():
        for ref in (dso_ref, dcq_ref, dco_ref, dew_ref, dcw_ref, dk_ref, dv_ref, dvec_ref):
            ref[...] = jnp.zeros_like(ref)

    def vec(name):
        row = ROW_OF[name]
        return vec_ref[row : row + 1, :]

    def add_vec(name, value):
        row = ROW_OF[name]
        dvec_ref[row : row + 1, :] += value

    context = ctx_ref[...]
    branch = dot_nn(context, so_ref[...]) + vec("sob")
    first_out, first_normed, first_inv = norm(
        x_ref[...].astype(F32) + branch, vec("g1"), vec("b1")
    )
    first_low = first_out.astype(BF)
    cross_q = (dot_nn(first_low, cq_ref[...]) + vec("cqb")).astype(BF)
    scaled_q = cross_q * jnp.asarray(0.125, BF)
    first_half = pair_masks(rows)
    zeros = jnp.zeros((rows, 128), BF)
    keys_count = k_ref.shape[0]
    top = lax.broadcasted_iota(jnp.int32, (128, keys_count), 0) < 64
    ones = jnp.ones((128, keys_count), BF)
    own_q, totals, contexts = [], [], []
    for pair in range(pairs):
        at = slice(pair * 128, pair * 128 + 128)
        key = k_ref[:, at]
        vt = v_ref[:, at].T
        parts = []
        for head in range(2):
            mine = first_half if head == 0 else ~first_half
            own = jnp.where(mine, scaled_q[:, at], zeros)
            scores = dot_nt(key, own)
            peak = jnp.max(scores, axis=0, keepdims=True)
            expd = jnp.exp(scores - peak).astype(BF)
            expd_ref[pair * 2 + head] = expd
            if head == 0:
                acc = dot_nn(jnp.where(top, vt, ones), expd)
                total = 1.0 / acc[64:65]
                parts.append(acc[:64] * total)
            else:
                acc = dot_nn(jnp.where(top, ones, vt), expd)
                total = 1.0 / acc[:1]
                parts.append(acc[64:] * total)
            own_q.append(own)
            totals.append(total)
        contexts.append(jnp.concatenate(parts, axis=0))
    context_t = jnp.concatenate(contexts, axis=0)
    cross_context = context_t.T.astype(BF)
    second_out, second_normed, second_inv = norm(
        first_out + dot_nn(cross_context, co_ref[...]) + vec("cob"), vec("g2"), vec("b2")
    )
    second_low = second_out.astype(BF)
    gate_bias = jnp.concatenate(
        [vec_ref[EB_ROW + j : EB_ROW + j + 1, :] for j in range(inner // width)], axis=1
    )
    gate_pre = dot_nn(second_low, ew_ref[...]) + gate_bias
    sig = 1.0 / (1.0 + jnp.exp(-gate_pre))
    silu = gate_pre * sig
    hidden = silu.astype(BF)
    slope = sig + silu * (1.0 - sig)
    final_out, third_normed, third_inv = norm(
        second_out + dot_nn(hidden, cw_ref[...]) + vec("cb"), vec("g3"), vec("b3")
    )
    out_ref[...] = final_out.astype(BF)

    incoming = cot_ref[...].astype(F32)
    add_vec("g3", col_sum(incoming * third_normed))
    add_vec("b3", col_sum(incoming))
    third_sum = norm_back(incoming, third_normed, third_inv, vec("g3"))
    branch_low = third_sum.astype(BF)
    dcw_ref[...] += dot_tn(hidden, branch_low)
    add_vec("cb", col_sum(branch_low))
    gate_low = (dot_nt(branch_low, cw_ref[...]) * slope).astype(BF)
    dew_ref[...] += dot_tn(second_low, gate_low)
    gate_sum = col_sum(gate_low)
    for j in range(inner // width):
        dvec_ref[EB_ROW + j : EB_ROW + j + 1, :] += gate_sum[:, j * width : (j + 1) * width]
    second_grad = third_sum + dot_nt(gate_low, ew_ref[...])
    add_vec("g2", col_sum(second_grad * second_normed))
    add_vec("b2", col_sum(second_grad))
    second_sum = norm_back(second_grad, second_normed, second_inv, vec("g2"))
    cross_low = second_sum.astype(BF)
    dco_ref[...] += dot_tn(cross_context, cross_low)
    add_vec("cob", col_sum(cross_low))
    grad_t = dot_nt(co_ref[...], cross_low)
    inner_t = grad_t * context_t
    dq_parts = []
    for pair in range(pairs):
        at = slice(pair * 128, pair * 128 + 128)
        key = k_ref[:, at]
        kt = key.T
        value = v_ref[:, at]
        scaled = jnp.concatenate(
            [
                grad_t[pair * 128 : pair * 128 + 64] * totals[pair * 2],
                grad_t[pair * 128 + 64 : pair * 128 + 128] * totals[pair * 2 + 1],
            ],
            axis=0,
        )
        grad = scaled.T.astype(BF)
        key_grad, value_grad, query_grad = [], [], []
        for head in range(2):
            mine = first_half if head == 0 else ~first_half
            own_grad = jnp.where(mine, grad, zeros)
            low = pair * 128 + head * 64
            delta = jnp.sum(inner_t[low : low + 64], axis=0, keepdims=True) * totals[
                pair * 2 + head
            ]
            expd = expd_ref[pair * 2 + head]
            score_low = (expd.astype(F32) * (dot_nt(value, own_grad) - delta)).astype(BF)
            query_grad.append(dot_nn(kt, score_low))
            key_grad.append(dot_nn(score_low, own_q[pair * 2 + head]))
            value_grad.append(dot_nn(expd, own_grad))
        dk_ref[:, at] += key_grad[0] + key_grad[1]
        dv_ref[:, at] += value_grad[0] + value_grad[1]
        dq_parts.append(query_grad[0][:64])
        dq_parts.append(query_grad[1][64:])
    cross_q_low = (jnp.concatenate(dq_parts, axis=0) * 0.125).T.astype(BF)
    dcq_ref[...] += dot_tn(first_low, cross_q_low)
    add_vec("cqb", col_sum(cross_q_low))
    first_grad = second_sum + dot_nt(cross_q_low, cq_ref[...])
    add_vec("g1", col_sum(first_grad * first_normed))
    add_vec("b1", col_sum(first_grad))
    first_sum = norm_back(first_grad, first_normed, first_inv, vec("g1"))
    fsg_ref[...] = first_sum
    self_low = first_sum.astype(BF)
    dso_ref[...] += dot_tn(context, self_low)
    add_vec("sob", col_sum(self_low))
    scl_ref[...] = dot_nt(self_low, so_ref[...]).astype(BF)


def middle(x, context, cotangent, cross_k, cross_v, so, cq, co, ew, cw, vecs):
    length, width = x.shape
    inner = ew.shape[1]
    block = pl.BlockSpec((ROWS, width), lambda i: (i, 0))

    def fixed(array):
        return pl.BlockSpec(array.shape, lambda i: (0,) * len(array.shape))

    square = jax.ShapeDtypeStruct((width, width), F32)
    mem = jax.ShapeDtypeStruct(cross_k.shape, F32)
    outs = [
        jax.ShapeDtypeStruct((length, width), BF),
        jax.ShapeDtypeStruct((length, width), F32),
        jax.ShapeDtypeStruct((length, width), BF),
        square, square, square,
        jax.ShapeDtypeStruct((width, inner), F32),
        jax.ShapeDtypeStruct((inner, width), F32),
        mem, mem,
        jax.ShapeDtypeStruct(vecs.shape, F32),
    ]
    weights = (cross_k, cross_v, so, cq, co, ew, cw, vecs)
    return pl.pallas_call(
        middle_kernel,
        grid=(length // ROWS,),
        in_specs=[block] * 3 + [
            pl.BlockSpec(w.shape, lambda i: (0, 0), pipeline_mode=pl.Buffered(1))
            for w in weights
        ],
        out_specs=[block] * 3 + [
            pl.BlockSpec(o.shape, lambda i: (0, 0), pipeline_mode=pl.Buffered(1))
            for o in outs[3:]
        ],
        out_shape=outs,
        scratch_shapes=[pltpu.VMEM((HEADS, cross_k.shape[0], ROWS), BF)],
        cost_estimate=pl.CostEstimate(
            flops=12 * length * width * inner + 60 * length * width * width,
            bytes_accessed=60 << 20,
            transcendentals=length * inner * 2 + length * cross_k.shape[0] * HEADS,
        ),
        name="middle",
    )(x, context, cotangent, *weights)


def local(n, *args):
    (
        decoder_in, memory, cotangent,
        self_query, self_query_bias, self_key, self_value, self_value_bias,
        self_output, self_output_bias, first_gain, first_shift,
        cross_query, cross_query_bias, cross_key, cross_value, cross_value_bias,
        cross_output, cross_output_bias, second_gain, second_shift,
        expand_weight, expand_bias, contract_weight, contract_bias,
        third_gain, third_shift,
    ) = args
    width = decoder_in.shape[1]
    small = self_query_bias.shape[0]
    rows = self_query.shape[0]
    inner = expand_weight.shape[1]
    wide = inner // width
    vectors = (
        self_query_bias, self_value_bias, self_output_bias, first_gain, first_shift,
        cross_query_bias, cross_value_bias, cross_output_bias, second_gain, second_shift,
        contract_bias, third_gain, third_shift,
    )
    count = len(vectors)
    packed = jnp.concatenate(vectors + (expand_bias,))
    pad = jnp.zeros((rows * width - packed.shape[0],), BF)
    packed = jnp.concatenate([packed, pad]).reshape(rows, width)

    got_self = gather_rows(
        jnp.concatenate([self_query, self_key, self_value, packed], axis=0), n
    )

    def whole(gathered, at, size):
        return gathered[:, at : at + size].reshape(n * size, width)

    full_sq = whole(got_self, 0, rows)
    full_sk = whole(got_self, rows, rows)
    full_sv = whole(got_self, 2 * rows, rows)
    flat = got_self[:, 3 * rows :].reshape(n, rows * width)
    table = flat[:, : count * small].reshape(n, count, small).transpose(1, 0, 2)
    table = table.reshape(count, width)
    gate_bias = flat[:, count * small : (count + wide) * small].reshape(wide, width)
    fill = jnp.zeros((-(count + wide) % 8, width), BF)
    vecs = jnp.concatenate([table, gate_bias, fill], axis=0).astype(F32)

    got_cross = gather_rows(
        jnp.concatenate(
            [self_output, cross_query, cross_key, cross_value, cross_output], axis=0
        ),
        n,
    )
    got_ffn = gather_rows(
        jnp.concatenate(
            [expand_weight[:, j * width : (j + 1) * width] for j in range(wide)]
            + [contract_weight],
            axis=0,
        ),
        n,
    )
    full_so, full_cq, full_ck, full_cv, full_co = [
        whole(got_cross, j * rows, rows) for j in range(5)
    ]
    full_ew = jnp.concatenate([whole(got_ffn, j * rows, rows) for j in range(wide)], axis=1)
    full_cw = whole(got_ffn, wide * rows, contract_weight.shape[0])

    query = (dot_nn(decoder_in, full_sq) + vecs[ROW_OF["sqb"]]).astype(BF)
    key = dot_nn(decoder_in, full_sk).astype(BF)
    value = (dot_nn(decoder_in, full_sv) + vecs[ROW_OF["svb"]]).astype(BF)
    context, log_sum = self_forward(query, key, value)
    cross_k = dot_nn(memory, full_ck).astype(BF)
    cross_v = (dot_nn(memory, full_cv) + vecs[ROW_OF["cvb"]]).astype(BF)
    (
        decoder_out, first_sum, context_low, dso, dcq, dco, dew, dcw, dck, dcv, dvec,
    ) = middle(
        decoder_in, context, cotangent, cross_k, cross_v,
        full_so, full_cq, full_co, full_ew, full_cw, vecs,
    )
    cross_k_low = dck.astype(BF)
    cross_v_low = dcv.astype(BF)
    memory_grad = dot_nt(cross_k_low, full_ck) + dot_nt(cross_v_low, full_cv)
    ck_grad = dot_tn(memory, cross_k_low)
    cv_grad = dot_tn(memory, cross_v_low)
    cvb_grad = jnp.sum(cross_v_low.astype(F32), axis=0)

    def split(grad):
        return grad.astype(BF).reshape(n, -1, width)

    def split_vec(rows_of):
        stacked = jnp.stack(rows_of).reshape(len(rows_of), n, small).transpose(1, 0, 2)
        flat = stacked.reshape(n, -1).astype(BF)
        pad = jnp.zeros((n, rows * width - flat.shape[1]), BF)
        return jnp.concatenate([flat, pad], axis=1).reshape(n, rows, width)

    names = ("sob", "g1", "b1", "cqb", "cob", "g2", "b2", "cb", "g3", "b3")
    vec_rows = [dvec[ROW_OF[name]] for name in names] + [cvb_grad]
    gate_flat = dvec[EB_ROW : EB_ROW + wide].reshape(n, wide * small)
    flat = jnp.stack(vec_rows).reshape(len(vec_rows), n, small).transpose(1, 0, 2)
    flat = jnp.concatenate([flat.reshape(n, -1), gate_flat], axis=1).astype(BF)
    vec_pad = jnp.zeros((n, rows * width - flat.shape[1]), BF)
    vec_block = jnp.concatenate([flat, vec_pad], axis=1).reshape(n, rows, width)
    mid = jnp.concatenate(
        [split(g) for g in (dso, dcq, ck_grad, cv_grad, dco)]
        + [split(dew[:, j * width : (j + 1) * width]) for j in range(wide)]
        + [split(dcw), vec_block],
        axis=1,
    )
    mid_sum = scatter_rows(mid, n)

    self_q_low, self_k_low, self_v_low = self_backward(
        query, key, value, context, context_low, log_sum
    )
    sq_grad = dot_tn(decoder_in, self_q_low)
    sk_grad = dot_tn(decoder_in, self_k_low)
    sv_grad = dot_tn(decoder_in, self_v_low)
    sqb_grad = jnp.sum(self_q_low.astype(F32), axis=0)
    svb_grad = jnp.sum(self_v_low.astype(F32), axis=0)
    last = jnp.concatenate(
        [split(g) for g in (sq_grad, sk_grad, sv_grad)] + [split_vec([sqb_grad, svb_grad])],
        axis=1,
    )
    last_sum = scatter_rows(last, n)
    input_grad = (
        first_sum
        + dot_nt(self_q_low, full_sq)
        + dot_nt(self_k_low, full_sk)
        + dot_nt(self_v_low, full_sv)
    )

    def take(total, at, size):
        return total[at : at + size]

    so_out, cq_out, ck_out, cv_out, co_out = [take(mid_sum, j * rows, rows) for j in range(5)]
    ew_out = jnp.concatenate(
        [take(mid_sum, (5 + j) * rows, rows) for j in range(wide)], axis=1
    )
    at = (5 + wide) * rows
    cw_out = take(mid_sum, at, contract_weight.shape[0])
    flat = mid_sum[at + contract_weight.shape[0] :].reshape(-1)
    vec_out = {
        name: flat[j * small : (j + 1) * small] for j, name in enumerate(names + ("cvb",))
    }
    at = (len(names) + 1) * small
    eb_out = flat[at : at + wide * small]
    flat = last_sum[3 * rows :].reshape(-1)
    sq_out, sk_out, sv_out = [take(last_sum, j * rows, rows) for j in range(3)]
    return (
        decoder_out, input_grad, memory_grad,
        sq_out, flat[:small], sk_out, sv_out, flat[small : 2 * small],
        so_out, vec_out["sob"], vec_out["g1"], vec_out["b1"],
        cq_out, vec_out["cqb"], ck_out, cv_out, vec_out["cvb"],
        co_out, vec_out["cob"], vec_out["g2"], vec_out["b2"],
        ew_out, eb_out, cw_out, vec_out["cb"], vec_out["g3"], vec_out["b3"],
    )


MATRICES = (0, 1, 2, 3, 5, 6, 8, 12, 14, 15, 17, 21, 23)


def solution(mesh):
    n = mesh.shape["fsdp"]
    specs = tuple(P("fsdp", None) if j in MATRICES else P("fsdp") for j in range(27))
    return jax.shard_map(
        functools.partial(local, n), mesh=mesh, in_specs=specs, out_specs=specs, check_vma=False
    )
```
